32 devices in a mesh: parts: 2 (over x), seq: 16 (over z, y, core).
Axes of the slice: x: 2, y: 2, z: 4, core: 2. Of those that a mesh axis runs over, the one named last changes fastest.
Arguments:
- queries: bfloat16 [3072, 1024], P(('parts', 'seq')), parts along dimension 0, may hold values from -8 to 8
- self_keys: bfloat16 [3072, 1024], P(('parts', 'seq')), parts along dimension 0, may hold values from -8 to 8
- self_values: bfloat16 [3072, 1024], P(('parts', 'seq')), parts along dimension 0, may hold values from -8 to 8
- residual_in: bfloat16 [3072, 1024], P(('parts', 'seq')), parts along dimension 0, may hold values from -0.23925781 to 0.23925781
- text_keys: bfloat16 [2, 8, 256, 1024], P(None, 'parts', None, 'seq'), parts along dimension 1, may hold values from -8 to 8
- text_values: bfloat16 [2, 8, 256, 1024], P(None, 'parts', None, 'seq'), parts along dimension 1, may hold values from -8 to 8
- text_lengths: int32 [2, 8], P(None, 'parts'), parts along dimension 1, may hold values from 2 to 256
- frame_counts: int32 [8], P('parts'), parts along dimension 0, may hold values from 1 to 16, 24 in all
- mod_gain: float32 [1024], replicated, may hold values from 0.1 to 1.9
- mod_shift: float32 [1024], replicated, may hold values from -1.8 to 1.8
- head_weight: bfloat16 [1024, 64], replicated, may hold values from -0.1875 to 0.1875
- head_bias: float32 [64], replicated, may hold values from -1.8 to 1.8
- guide_scale: float32 [1], replicated, may hold values from 3 to 7
Outputs:
- guided: float32 [1536, 64], P(('parts', 'seq')), parts along dimension 0
The draws below stay inside these ranges and needn't reach their ends.
There are 2 independent parts, one for each index of `parts`. The reference program is written for one: setup_inputs(seed, part) draws one part's arguments, and reference() takes and returns one part's arrays. A program takes and returns all parts, laid end to end along the dimension named above; an argument that names none is the same for every part. Nothing has to cross between parts.
Inputs may be any that keep to these rules, and one draw needn't show every extreme that they name: `frame_counts`: latent frames of the 4 videos in packing order; they sum to 24 and the largest is exactly 16. `text_lengths`: live prompt tokens, counted from the front of each prompt.
All inputs are finite; a program needn't handle non-finite values.
Results may differ from the reference program's by a relative error of at most 0.0049.
Values may be sent and summed in bfloat16 or wider, within the bound.
A program may use at most 64 MiB of HBM per device.

```python
import math
import jax
import jax.numpy as jnp
import numpy as np
from jax import lax

HEAD_CHANNELS = 128
HEADS = 8
D = 1024
OUT = 64
TOK_DEV = 96
TPF = 32
TEXT = 256
VIDEOS = 4
TOKENS = 768
LATENT_FRAMES = 24
MAX_FRAMES = 16


def clipped_normal(key, shape):
    return jnp.clip(jax.random.normal(key, shape, jnp.float32), -8.0, 8.0)


def draw_queries(key, part):
    value_rows = clipped_normal(jax.random.fold_in(key, 11), (2 * TOKENS, D))
    return value_rows.astype(jnp.bfloat16)


def draw_self_keys(key, part):
    value_rows = clipped_normal(jax.random.fold_in(key, 12), (2 * TOKENS, D))
    return value_rows.astype(jnp.bfloat16)


def draw_text_keys(key, part):
    value_rows = clipped_normal(jax.random.fold_in(key, 13), (2, VIDEOS, TEXT, D))
    return value_rows.astype(jnp.bfloat16)


def with_ends(values, rng, least, top_value):
    dims = values.shape
    index_at = [jax.random.randint(jax.random.fold_in(rng, axis), (), 0, dims[axis]) for axis in range(len(dims))]
    values = values.at[tuple(index_at)].set(least)
    longest = dims.index(max(dims))
    index_at[longest] = (index_at[longest] + 1) % dims[longest]
    return values.at[tuple(index_at)].set(top_value)


def level_of(own_key, shape, shards, smallest, high):
    def one(dim, shards_of):
        heights = jax.random.uniform(jax.random.fold_in(jax.random.fold_in(own_key, 6), dim), (shards_of,), jnp.float32, smallest / len(shards), high / len(shards))
        return jnp.repeat(jnp.exp(heights), shape[dim] // shards_of).reshape((-1,) + (1,) * (len(shape) - dim - 1))

    loudness = one(*shards[0])
    for cut in shards[1:]:
        loudness = loudness * one(*cut)
    return loudness


def split_up(number_of, total, limit, slope):
    weights = [(1 << 20) // math.isqrt(rank ** slope) + 1 for rank in range(2, number_of + 1)]
    spare, counts = total - limit - (number_of - 1), [1] * (number_of - 1)
    while spare > 0:
        movable = [i for i in range(number_of - 1) if counts[i] < limit]
        mass, budget = sum([weights[i] for i in movable]), spare
        for i in movable:
            more = min(limit - counts[i], max(1, budget * weights[i] // mass), spare)
            counts[i] = counts[i] + more
            spare = spare - more
    return np.array([limit] + counts)


def ragged_sizes(rng, amount, total, reach, lean):
    if amount == 2:
        one = jax.random.randint(rng, (), max(1, total - reach), min(reach, total - 1) + 1)
        return jnp.stack([one, total - one])
    lengths = jnp.asarray(split_up(amount, total, reach, lean), jnp.int32)
    couples = (amount - 1) // 2
    source_of, sink = lengths[1:1 + 2 * couples:2], lengths[2:2 + 2 * couples:2]
    margin = jnp.minimum(source_of - 1, reach - sink)
    passed = jax.random.randint(jax.random.fold_in(rng, 1), (couples,), 0, 1 << 20) % (margin + 1)
    lengths = lengths.at[1:1 + 2 * couples:2].set(source_of - passed).at[2:2 + 2 * couples:2].set(sink + passed)
    return lengths[jax.random.permutation(jax.random.fold_in(rng, 2), amount)]


def gaussian(stream_key, shape, scale, limit, shards=(), kind=jnp.bfloat16):
    drawn = jax.random.normal(stream_key, shape, jnp.float32) * scale
    if len(shards) > 0:
        drawn = level_of(stream_key, shape, shards, -0.22, 0.18) * drawn
    return jnp.clip(drawn, min=-limit, max=limit).astype(kind)


def setup_inputs(seed: int = 0, part: int = 0) -> dict:
    key_list = jax.random.split(jax.random.key(seed), 14)
    part_splits = jax.random.split(jax.random.fold_in(key_list[13], part), 14)
    queries = draw_queries(jax.random.fold_in(jax.random.fold_in(key_list[13], part), 71), part)
    self_keys = draw_self_keys(jax.random.fold_in(jax.random.fold_in(key_list[13], part), 71), part)
    self_values = gaussian(part_splits[2], (2 * TOKENS, D), 1.0, 8.0, ((0, 16),))
    residual_in = gaussian(part_splits[3], (2 * TOKENS, D), 0.03, 0.23925781, ((0, 16),))
    text_keys = draw_text_keys(jax.random.fold_in(jax.random.fold_in(key_list[13], part), 71), part)
    text_values = gaussian(part_splits[5], (2, VIDEOS, TEXT, D), 1.0, 8.0, ((3, 16),))
    text_lengths = with_ends(jax.random.randint(part_splits[6], (2, VIDEOS), 2, TEXT + 1), jax.random.fold_in(part_splits[6], 1), 2, TEXT).astype(jnp.int32)
    frame_counts = ragged_sizes(part_splits[7], VIDEOS, LATENT_FRAMES, MAX_FRAMES, 2).astype(jnp.int32)
    mod_gain = jnp.clip(1.0 + 0.18 * jax.random.normal(key_list[8], (D,), jnp.float32), 0.1, 1.9)
    mod_shift = gaussian(key_list[9], (D,), 0.3, 1.8, (), jnp.float32)
    head_weight = gaussian(key_list[10], (D, OUT), D ** -0.5, 0.1875)
    head_bias = gaussian(key_list[11], (OUT,), 0.3, 1.8, (), jnp.float32)
    guide_scale = jnp.clip(jax.random.uniform(key_list[12], (1,), jnp.float32, 3.0, 7.0), 3.0, 7.0)
    return {"queries": queries, "self_keys": self_keys, "self_values": self_values, "residual_in": residual_in, "text_keys": text_keys, "text_values": text_values, "text_lengths": text_lengths, "frame_counts": frame_counts, "mod_gain": mod_gain, "mod_shift": mod_shift, "head_weight": head_weight, "head_bias": head_bias, "guide_scale": guide_scale}


def branch_major(packed):
    features = packed.shape[1]
    device_slices = packed.shape[0] // (2 * TOK_DEV)
    grouped = packed.reshape(device_slices, 2, TOK_DEV, features)
    return grouped.transpose(1, 0, 2, 3).reshape(2, device_slices * TOK_DEV, features)

def by_heads(arranged):
    return arranged.reshape(2, arranged.shape[1], HEADS, HEAD_CHANNELS).transpose(2, 0, 1, 3)

def soft_attend(queries, incoming_keys, value_rows, allowed):
    logit_scores = jnp.einsum('pag,pmg->pam', queries.astype(jnp.float32), incoming_keys.astype(jnp.float32)) * HEAD_CHANNELS ** (-0.5)
    logit_scores = jnp.where(allowed, logit_scores, -1e+30)
    row_max = lax.optimization_barrier(jnp.max(logit_scores, axis=-1, keepdims=True))
    raised = jnp.exp(logit_scores - row_max)
    softmax_weights = (raised / lax.optimization_barrier(jnp.sum(raised, axis=-1, keepdims=True))).astype(jnp.bfloat16)
    return jnp.einsum('ehm,emp->ehp', softmax_weights.astype(jnp.float32), value_rows.astype(jnp.float32))

def reference(queries, self_keys, self_values, residual_in, text_keys, text_values, text_lengths, frame_counts, mod_gain, mod_shift, head_weight, head_bias, guide_scale):
    video_ends = jnp.cumsum(frame_counts.astype(jnp.int32)) * TPF
    positions = jnp.arange(TOKENS, dtype=jnp.int32)
    video_ids = lax.optimization_barrier(jnp.sum((positions[:, None] >= video_ends[None, :]).astype(jnp.int32), axis=1))
    self_allowed = (video_ids[:, None] == video_ids[None, :])[None]
    text_slots = jnp.arange(VIDEOS * TEXT, dtype=jnp.int32)
    slot_video = text_slots // TEXT
    slot_place = text_slots % TEXT
    live_slot = slot_place[None, :] < text_lengths.astype(jnp.int32)[:, slot_video]
    cross_allowed = (video_ids[None, :, None] == slot_video[None, None, :]) & live_slot[:, None, :]
    operands = (by_heads(branch_major(queries)), by_heads(branch_major(self_keys)), by_heads(branch_major(self_values)), by_heads(text_keys.reshape(2, VIDEOS * TEXT, D)), by_heads(text_values.reshape(2, VIDEOS * TEXT, D)))

    def per_head(pieces):
        head_query, head_key, head_value, head_tkey, head_tvalue = pieces
        combined = soft_attend(head_query, head_key, head_value, self_allowed) + soft_attend(head_query, head_tkey, head_tvalue, cross_allowed)
        return combined.astype(jnp.bfloat16)
    attention = lax.map(per_head, operands)
    attention = attention.transpose(1, 2, 0, 3).reshape(2, TOKENS, D)
    hidden = branch_major(residual_in).astype(jnp.float32) + attention.astype(jnp.float32)
    row_mean = lax.optimization_barrier(jnp.mean(hidden, axis=-1, keepdims=True))
    centred = hidden - row_mean
    row_var = lax.optimization_barrier(jnp.mean(centred * centred, axis=-1, keepdims=True))
    normed = (centred * lax.rsqrt(row_var + 1e-06) * mod_gain + mod_shift).astype(jnp.bfloat16)
    velocity = jnp.dot(normed.reshape(2 * TOKENS, D), head_weight, preferred_element_type=jnp.float32).reshape(2, TOKENS, OUT) + head_bias
    return velocity[1] + guide_scale[0] * (velocity[0] - velocity[1])
```

```python
import functools
import math

import jax
import jax.numpy as jnp
from jax import lax
from jax.experimental import pallas as pl
from jax.experimental.pallas import tpu as pltpu
from jax.sharding import PartitionSpec as P

HEAD_CHANNELS = 128
TPF = 32
PENALTY = -1e30
EXP_SCALE = HEAD_CHANNELS ** (-0.5) * math.log2(math.e)
MESH_ID = pl.DeviceIdType.MESH


def inside(rows, starts, ends):
    lane = lax.broadcasted_iota(jnp.int32, (1, HEAD_CHANNELS), 1)
    low = jnp.zeros((1, HEAD_CHANNELS), jnp.int32)
    high = jnp.zeros((1, HEAD_CHANNELS), jnp.int32)
    for f, (start, end) in enumerate(zip(starts, ends)):
        low = jnp.where(lane == f, start, low)
        high = jnp.where(lane == f, end, high)
    row = lax.broadcasted_iota(jnp.int32, (rows, HEAD_CHANNELS), 0)
    return (row >= low) & (row < high)


def weights_of(queries, keys):
    scores = lax.dot_general(
        queries, keys, (((1,), (1,)), ((), ())), preferred_element_type=jnp.float32
    )
    top = jnp.max(scores, axis=-1, keepdims=True)
    raised = jnp.exp2((scores - top) * EXP_SCALE)
    total = jnp.sum(raised, axis=-1, keepdims=True)
    return (raised * (1.0 / total)).astype(jnp.bfloat16)


def kernel(
    n,
    q_ref,
    k_ref,
    v_ref,
    x_ref,
    tk_ref,
    tv_ref,
    lengths_ref,
    frames_ref,
    gain_ref,
    shift_ref,
    weight_ref,
    bias_ref,
    out_ref,
    qb,
    kb,
    vb,
    q_hot,
    k_pen,
    tkb,
    tvb,
    t_keys,
    t_vals,
    p_self,
    cross,
    ob,
    att,
    xb,
    qkv_send,
    qkv_recv,
    pair_send,
    pair_recv,
    out_send,
    out_recv,
    here_sem,
):
    me = lax.axis_index("seq")
    chips = n // 2
    chip, core = me // 2, me % 2
    partner = chip * 2 + (1 - core)
    rows = q_ref.shape[0]
    half = rows // 2
    tokens = chips * rows
    videos = frames_ref.shape[0]
    slots = tk_ref.shape[1]
    text = slots // videos
    sources = (q_ref, k_ref, v_ref)
    landings = (qb, kb, vb)

    def block(index, size):
        return pl.ds(pl.multiple_of(index * size, size), size)

    def qkv_copy(which, peer):
        return pltpu.make_async_remote_copy(
            src_ref=sources[which].at[:, block(peer, HEAD_CHANNELS)],
            dst_ref=landings[which].at[block(chip, rows)],
            send_sem=qkv_send.at[which, peer],
            recv_sem=qkv_recv.at[which, chip],
            device_id={"seq": peer * 2 + core},
            device_id_type=MESH_ID,
        )

    def own_copy(which):
        return pltpu.make_async_copy(
            sources[which].at[:, block(chip, HEAD_CHANNELS)],
            landings[which].at[block(chip, rows)],
            qkv_recv.at[which, chip],
        )

    def qkv_wait(which, peer):
        place = landings[which].at[block(peer, rows)]
        pltpu.make_async_copy(place, place, qkv_recv.at[which, peer]).wait()

    pair_parts = (
        (tk_ref.at[1 - core], tkb.at[core]),
        (tv_ref.at[1 - core], tvb.at[core]),
        (x_ref.at[block(1 - core, half)], xb.at[core]),
    )
    here_parts = (
        (tk_ref.at[core], tkb.at[core]),
        (tv_ref.at[core], tvb.at[core]),
        (x_ref.at[block(core, half)], xb.at[core]),
    )
    pair_copies = [
        pltpu.make_async_remote_copy(
            src_ref=source,
            dst_ref=landing,
            send_sem=pair_send.at[i],
            recv_sem=pair_recv.at[i],
            device_id={"seq": partner},
            device_id_type=MESH_ID,
        )
        for i, (source, landing) in enumerate(pair_parts)
    ]
    here_copies = [
        pltpu.make_async_copy(source, landing, here_sem.at[i])
        for i, (source, landing) in enumerate(here_parts)
    ]

    barrier = pltpu.get_barrier_semaphore()

    @pl.loop(1, n)
    def _(step):
        pl.semaphore_signal(
            barrier, inc=1, device_id={"seq": lax.rem(me + step, n)}, device_id_type=MESH_ID
        )

    for copy in here_copies:
        copy.start()
    for which in range(3):
        own_copy(which).start()

    pl.semaphore_wait(barrier, n - 1)

    pair_copies[0].start()
    for which in range(3):

        @pl.loop(1, chips)
        def _(step, which=which):
            qkv_copy(which, lax.rem(chip + step, chips)).start()

        if which < 2:
            pair_copies[which + 1].start()

    starts, ends, position = [], [], jnp.int32(0)
    for f in range(videos):
        starts.append(position)
        position = position + frames_ref[f] * TPF
        ends.append(position)
    same = inside(tokens, starts, ends)
    q_hot[...] = jnp.where(same, 1.0, 0.0).astype(jnp.bfloat16)
    k_pen[...] = jnp.where(same, 0.0, PENALTY).astype(jnp.bfloat16)
    lengths = [
        jnp.where(core == 0, lengths_ref[0, f], lengths_ref[1, f]) for f in range(videos)
    ]
    live = inside(
        slots, [f * text for f in range(videos)], [f * text + lengths[f] for f in range(videos)]
    )
    t_keys[:, HEAD_CHANNELS:] = jnp.where(live, 0.0, PENALTY).astype(jnp.bfloat16)

    def pair_wait(i):
        here_copies[i].wait()
        pair_copies[i].wait_recv()

    pair_wait(0)
    t_keys[:, :HEAD_CHANNELS] = jnp.concatenate([tkb[0], tkb[1]], axis=-1)
    pair_wait(1)
    t_vals[...] = jnp.concatenate([tvb[0], tvb[1]], axis=-1)

    def query_block(index):
        place = block(index, rows)
        return jnp.concatenate([qb[place, :], q_hot[place, :]], axis=-1)

    @pl.loop(0, chips)
    def _(step):
        index = lax.rem(chip + step, chips)
        qkv_wait(0, index)
        weights = weights_of(query_block(index), t_keys[...])
        cross[block(index, rows), :] = jnp.dot(
            weights, t_vals[...], preferred_element_type=jnp.float32
        )

    @pl.loop(0, chips)
    def _(step):
        qkv_wait(1, step)

    @pl.loop(0, chips)
    def _(step):
        index = lax.rem(chip + step, chips)
        keys = jnp.concatenate([kb[...], k_pen[...]], axis=-1)
        p_self[block(index, rows), :] = weights_of(query_block(index), keys)

    @pl.loop(0, chips)
    def _(step):
        qkv_wait(2, step)

    def out_copy(device):
        return pltpu.make_async_remote_copy(
            src_ref=ob.at[block(device, half)],
            dst_ref=att.at[core, :, block(chip, HEAD_CHANNELS)],
            send_sem=out_send.at[device],
            recv_sem=out_recv.at[me],
            device_id={"seq": device},
            device_id_type=MESH_ID,
        )

    def out_own():
        return pltpu.make_async_copy(
            ob.at[block(me, half)],
            att.at[core, :, block(chip, HEAD_CHANNELS)],
            out_recv.at[me],
        )

    @pl.loop(0, chips)
    def _(step):
        index = lax.rem(chip + 1 + step, chips)
        place = block(index, rows)
        mixed = cross[place, :] + jnp.dot(
            p_self[place, :], vb[...], preferred_element_type=jnp.float32
        )
        ob[place, :] = mixed.astype(jnp.bfloat16)
        for side in range(2):
            device = index * 2 + side

            @pl.when(device != me)
            def _():
                out_copy(device).start()

            @pl.when(device == me)
            def _():
                out_own().start()

    pair_wait(2)

    @pl.loop(0, n)
    def _(device):
        place = att.at[device % 2, :, block(device // 2, HEAD_CHANNELS)]
        pltpu.make_async_copy(place, place, out_recv.at[device]).wait()

    features = x_ref.shape[1]
    hidden = (xb[...].astype(jnp.float32) + att[...].astype(jnp.float32)).reshape(rows, features)
    centred = hidden - jnp.mean(hidden, axis=-1, keepdims=True)
    spread = jnp.mean(centred * centred, axis=-1, keepdims=True)
    normed = centred * lax.rsqrt(spread + 1e-06) * gain_ref[...] + shift_ref[...]
    velocity = (
        jnp.dot(normed.astype(jnp.bfloat16), weight_ref[...], preferred_element_type=jnp.float32)
        + bias_ref[...]
    )
    out_ref[...] = velocity

    for copy in pair_copies:
        copy.wait_send()
    for which in range(3):

        @pl.loop(1, chips)
        def _(step, which=which):
            qkv_copy(which, lax.rem(chip + step, chips)).wait_send()

    @pl.loop(1, n)
    def _(step):
        out_copy(lax.rem(me + step, n)).wait_send()


def local(
    queries,
    self_keys,
    self_values,
    residual_in,
    text_keys,
    text_values,
    text_lengths,
    frame_counts,
    mod_gain,
    mod_shift,
    head_weight,
    head_bias,
    guide_scale,
):
    n = lax.axis_size("seq")
    chips = n // 2
    rows, features = queries.shape
    half = rows // 2
    outs = head_weight.shape[1]
    tokens = chips * rows
    branches, videos, text, share = text_keys.shape
    slots = videos * text
    bf16, f32 = jnp.bfloat16, jnp.float32
    anywhere = pl.BlockSpec(memory_space=pl.ANY)
    scalar = pl.BlockSpec(memory_space=pltpu.SMEM)
    vector = pl.BlockSpec(memory_space=pltpu.VMEM)
    velocity = pl.pallas_call(
        functools.partial(kernel, n),
        out_shape=jax.ShapeDtypeStruct((rows, outs), f32),
        in_specs=[anywhere] * 6 + [scalar] * 2 + [vector] * 4,
        out_specs=vector,
        scratch_shapes=[
            pltpu.VMEM((tokens, HEAD_CHANNELS), bf16),
            pltpu.VMEM((tokens, HEAD_CHANNELS), bf16),
            pltpu.VMEM((tokens, HEAD_CHANNELS), bf16),
            pltpu.VMEM((tokens, HEAD_CHANNELS), bf16),
            pltpu.VMEM((tokens, HEAD_CHANNELS), bf16),
            pltpu.VMEM((2, slots, share), bf16),
            pltpu.VMEM((2, slots, share), bf16),
            pltpu.VMEM((slots, 2 * HEAD_CHANNELS), bf16),
            pltpu.VMEM((slots, HEAD_CHANNELS), bf16),
            pltpu.VMEM((tokens, tokens), bf16),
            pltpu.VMEM((tokens, HEAD_CHANNELS), f32),
            pltpu.VMEM((tokens, HEAD_CHANNELS), bf16),
            pltpu.VMEM((2, half, features), bf16),
            pltpu.VMEM((2, half, features), bf16),
            pltpu.SemaphoreType.DMA((3, chips)),
            pltpu.SemaphoreType.DMA((3, chips)),
            pltpu.SemaphoreType.DMA((3,)),
            pltpu.SemaphoreType.DMA((3,)),
            pltpu.SemaphoreType.DMA((n,)),
            pltpu.SemaphoreType.DMA((n,)),
            pltpu.SemaphoreType.DMA((3,)),
        ],
        compiler_params=pltpu.CompilerParams(
            collective_id=0, has_side_effects=True, vmem_limit_bytes=60 * 1024 * 1024
        ),
        name="guided_block",
    )(
        queries,
        self_keys,
        self_values,
        residual_in,
        text_keys.reshape(branches, slots, share),
        text_values.reshape(branches, slots, share),
        text_lengths,
        frame_counts,
        mod_gain.reshape(1, features),
        mod_shift.reshape(1, features),
        head_weight,
        head_bias.reshape(1, outs),
    )
    conditional, unconditional = velocity[:half], velocity[half:]
    return unconditional + guide_scale[0] * (conditional - unconditional)


def solution(mesh):
    return jax.shard_map(
        local,
        mesh=mesh,
        in_specs=(
            P(("parts", "seq"), None),
            P(("parts", "seq"), None),
            P(("parts", "seq"), None),
            P(("parts", "seq"), None),
            P(None, "parts", None, "seq"),
            P(None, "parts", None, "seq"),
            P(None, "parts"),
            P("parts"),
            P(),
            P(),
            P(),
            P(),
            P(),
        ),
        out_specs=P(("parts", "seq"), None),
        check_vma=False,
    )
```

```python
import functools
import math

import jax
import jax.numpy as jnp
from jax import lax
from jax.experimental import pallas as pl
from jax.experimental.pallas import tpu as pltpu
from jax.sharding import PartitionSpec as P

HEAD_CHANNELS = 128
TPF = 32
PENALTY = -1e30
EXP_SCALE = HEAD_CHANNELS ** (-0.5) * math.log2(math.e)
MESH_ID = pl.DeviceIdType.MESH


def inside(shape, dim, starts, ends):
    thin = tuple(1 if i == dim else size for i, size in enumerate(shape))
    feature = lax.broadcasted_iota(jnp.int32, thin, 1 - dim)
    low = jnp.zeros(thin, jnp.int32)
    high = jnp.zeros(thin, jnp.int32)
    for f, (start, end) in enumerate(zip(starts, ends)):
        low = jnp.where(feature == f, start, low)
        high = jnp.where(feature == f, end, high)
    place = lax.broadcasted_iota(jnp.int32, shape, dim)
    return (place >= low) & (place < high)


def weights_of(scores):
    top = jnp.max(scores, axis=-1, keepdims=True)
    raised = jnp.exp2((scores - top) * EXP_SCALE)
    total = jnp.sum(raised, axis=-1, keepdims=True)
    return (raised * (1.0 / total)).astype(jnp.bfloat16)


def kernel(
    n,
    q_ref,
    k_ref,
    v_ref,
    x_ref,
    tk_ref,
    tv_ref,
    lengths_ref,
    frames_ref,
    gain_ref,
    shift_ref,
    weight_ref,
    bias_ref,
    guide_ref,
    out_ref,
    qb,
    kb,
    vb,
    q_hot,
    keys,
    t_keys,
    t_vals_in,
    t_vals,
    p_self,
    cross,
    ob,
    att,
    xb,
    qkv_send,
    qkv_recv,
    pair_send,
    pair_recv,
    out_send,
    out_recv,
    here_sem,
):
    me = lax.axis_index("seq")
    chips = n // 2
    chip, core = me // 2, me % 2
    partner = chip * 2 + (1 - core)
    rows = q_ref.shape[0]
    half = rows // 2
    tokens = chips * rows
    videos = frames_ref.shape[0]
    share, text = tk_ref.shape[2:]
    sources = (q_ref, k_ref, v_ref)
    landings = (qb, kb, vb)

    def block(index, size):
        return pl.ds(pl.multiple_of(index * size, size), size)

    def qkv_copy(which, peer):
        return pltpu.make_async_remote_copy(
            src_ref=sources[which].at[:, block(peer, HEAD_CHANNELS)],
            dst_ref=landings[which].at[block(chip, rows)],
            send_sem=qkv_send.at[which, peer],
            recv_sem=qkv_recv.at[which, chip],
            device_id={"seq": peer * 2 + core},
            device_id_type=MESH_ID,
        )

    def own_copy(which):
        return pltpu.make_async_copy(
            sources[which].at[:, block(chip, HEAD_CHANNELS)],
            landings[which].at[block(chip, rows)],
            qkv_recv.at[which, chip],
        )

    def qkv_wait(which, peer):
        place = landings[which].at[block(peer, rows)]
        pltpu.make_async_copy(place, place, qkv_recv.at[which, peer]).wait()

    key_place = t_keys.at[:, block(core, share), :]
    value_place = t_vals_in.at[:, block(core, share), :]
    pair_parts = (
        (tk_ref.at[1 - core], key_place),
        (tv_ref.at[1 - core], value_place),
        (x_ref.at[block(1 - core, half)], xb.at[core]),
    )
    here_parts = (
        (tk_ref.at[core], key_place),
        (tv_ref.at[core], value_place),
        (x_ref.at[block(core, half)], xb.at[core]),
    )
    pair_copies = [
        pltpu.make_async_remote_copy(
            src_ref=source,
            dst_ref=landing,
            send_sem=pair_send.at[i],
            recv_sem=pair_recv.at[i],
            device_id={"seq": partner},
            device_id_type=MESH_ID,
        )
        for i, (source, landing) in enumerate(pair_parts)
    ]
    here_copies = [
        pltpu.make_async_copy(source, landing, here_sem.at[i])
        for i, (source, landing) in enumerate(here_parts)
    ]

    barrier = pltpu.get_barrier_semaphore()

    @pl.loop(1, n)
    def _(step):
        pl.semaphore_signal(
            barrier, inc=1, device_id={"seq": lax.rem(me + step, n)}, device_id_type=MESH_ID
        )

    for copy in here_copies:
        copy.start()
    for which in range(3):
        own_copy(which).start()

    pl.semaphore_wait(barrier, n - 1)

    pair_copies[0].start()
    for which in range(3):

        @pl.loop(1, chips)
        def _(step, which=which):
            qkv_copy(which, lax.rem(chip + step, chips)).start()

        if which < 2:
            pair_copies[which + 1].start()

    starts, ends, position = [], [], jnp.int32(0)
    for f in range(videos):
        starts.append(position)
        position = position + frames_ref[f] * TPF
        ends.append(position)
    same = inside((tokens, HEAD_CHANNELS), 0, starts, ends)
    q_hot[...] = jnp.where(same, 1.0, 0.0).astype(jnp.bfloat16)
    apart = ~inside((HEAD_CHANNELS, tokens), 1, starts, ends)
    keys[HEAD_CHANNELS:, :] = jnp.where(apart, PENALTY, 0.0).astype(jnp.bfloat16)
    for f in range(videos):
        length = jnp.where(core == 0, lengths_ref[0, f], lengths_ref[1, f])
        live = inside(
            (HEAD_CHANNELS, text),
            1,
            [0] * videos,
            [length if other == f else 0 for other in range(videos)],
        )
        t_keys[f, HEAD_CHANNELS:, :] = jnp.where(live, 0.0, PENALTY).astype(jnp.bfloat16)

    def pair_wait(i):
        here_copies[i].wait()
        pair_copies[i].wait_recv()

    pair_wait(0)
    pair_wait(1)
    for f in range(videos):
        t_vals[f * text : (f + 1) * text, :] = t_vals_in[f].T

    def query_block(index):
        place = block(index, rows)
        return jnp.concatenate([qb[place, :], q_hot[place, :]], axis=-1)

    @pl.loop(0, chips)
    def _(step):
        index = lax.rem(chip + step, chips)
        qkv_wait(0, index)
        queries = query_block(index)
        scores = jnp.concatenate(
            [
                jnp.dot(queries, t_keys[f], preferred_element_type=jnp.float32)
                for f in range(videos)
            ],
            axis=-1,
        )
        weights = weights_of(scores)
        cross[block(index, rows), :] = jnp.dot(
            weights, t_vals[...], preferred_element_type=jnp.float32
        )

    @pl.loop(0, chips)
    def _(step):
        qkv_wait(1, step)

    keys[:HEAD_CHANNELS, :] = kb[...].T

    @pl.loop(0, chips)
    def _(step):
        index = lax.rem(chip + step, chips)
        scores = jnp.dot(query_block(index), keys[...], preferred_element_type=jnp.float32)
        p_self[block(index, rows), :] = weights_of(scores)

    @pl.loop(0, chips)
    def _(step):
        qkv_wait(2, step)

    def out_copy(device):
        return pltpu.make_async_remote_copy(
            src_ref=ob.at[block(device, half)],
            dst_ref=att.at[core, :, block(chip, HEAD_CHANNELS)],
            send_sem=out_send.at[device],
            recv_sem=out_recv.at[me],
            device_id={"seq": device},
            device_id_type=MESH_ID,
        )

    def out_own():
        return pltpu.make_async_copy(
            ob.at[block(me, half)],
            att.at[core, :, block(chip, HEAD_CHANNELS)],
            out_recv.at[me],
        )

    @pl.loop(0, chips)
    def _(step):
        index = lax.rem(chip + 1 + step, chips)
        place = block(index, rows)
        mixed = cross[place, :] + jnp.dot(
            p_self[place, :], vb[...], preferred_element_type=jnp.float32
        )
        ob[place, :] = mixed.astype(jnp.bfloat16)
        for side in range(2):
            device = index * 2 + side

            @pl.when(device != me)
            def _():
                out_copy(device).start()

            @pl.when(device == me)
            def _():
                out_own().start()

    pair_wait(2)

    @pl.loop(0, n)
    def _(device):
        place = att.at[device % 2, :, block(device // 2, HEAD_CHANNELS)]
        pltpu.make_async_copy(place, place, out_recv.at[device]).wait()

    features = x_ref.shape[1]
    hidden = (xb[...].astype(jnp.float32) + att[...].astype(jnp.float32)).reshape(rows, features)
    centred = hidden - jnp.mean(hidden, axis=-1, keepdims=True)
    spread = jnp.mean(centred * centred, axis=-1, keepdims=True)
    normed = centred * lax.rsqrt(spread + 1e-06) * gain_ref[...] + shift_ref[...]
    velocity = (
        lax.dot_general(
            normed.astype(jnp.bfloat16),
            weight_ref[...],
            (((1,), (1,)), ((), ())),
            preferred_element_type=jnp.float32,
        )
        + bias_ref[...]
    )
    conditional, unconditional = velocity[:half], velocity[half:]
    out_ref[...] = unconditional + guide_ref[0] * (conditional - unconditional)

    for copy in pair_copies:
        copy.wait_send()
    for which in range(3):

        @pl.loop(1, chips)
        def _(step, which=which):
            qkv_copy(which, lax.rem(chip + step, chips)).wait_send()

    @pl.loop(1, n)
    def _(step):
        out_copy(lax.rem(me + step, n)).wait_send()


def local(
    queries,
    self_keys,
    self_values,
    residual_in,
    text_keys,
    text_values,
    text_lengths,
    frame_counts,
    mod_gain,
    mod_shift,
    head_weight,
    head_bias,
    guide_scale,
):
    n = lax.axis_size("seq")
    chips = n // 2
    rows, features = queries.shape
    half = rows // 2
    outs = head_weight.shape[1]
    tokens = chips * rows
    _, videos, text, _ = text_keys.shape
    bf16, f32 = jnp.bfloat16, jnp.float32
    anywhere = pl.BlockSpec(memory_space=pl.ANY)
    scalar = pl.BlockSpec(memory_space=pltpu.SMEM)
    vector = pl.BlockSpec(memory_space=pltpu.VMEM)
    return pl.pallas_call(
        functools.partial(kernel, n),
        out_shape=jax.ShapeDtypeStruct((half, outs), f32),
        in_specs=[anywhere] * 6 + [scalar] * 2 + [vector] * 4 + [scalar],
        out_specs=vector,
        scratch_shapes=[
            pltpu.VMEM((tokens, HEAD_CHANNELS), bf16),
            pltpu.VMEM((tokens, HEAD_CHANNELS), bf16),
            pltpu.VMEM((tokens, HEAD_CHANNELS), bf16),
            pltpu.VMEM((tokens, HEAD_CHANNELS), bf16),
            pltpu.VMEM((2 * HEAD_CHANNELS, tokens), bf16),
            pltpu.VMEM((videos, 2 * HEAD_CHANNELS, text), bf16),
            pltpu.VMEM((videos, HEAD_CHANNELS, text), bf16),
            pltpu.VMEM((videos * text, HEAD_CHANNELS), bf16),
            pltpu.VMEM((tokens, tokens), bf16),
            pltpu.VMEM((tokens, HEAD_CHANNELS), f32),
            pltpu.VMEM((tokens, HEAD_CHANNELS), bf16),
            pltpu.VMEM((2, half, features), bf16),
            pltpu.VMEM((2, half, features), bf16),
            pltpu.SemaphoreType.DMA((3, chips)),
            pltpu.SemaphoreType.DMA((3, chips)),
            pltpu.SemaphoreType.DMA((3,)),
            pltpu.SemaphoreType.DMA((3,)),
            pltpu.SemaphoreType.DMA((n,)),
            pltpu.SemaphoreType.DMA((n,)),
            pltpu.SemaphoreType.DMA((3,)),
        ],
        compiler_params=pltpu.CompilerParams(
            collective_id=0, has_side_effects=True, vmem_limit_bytes=60 * 1024 * 1024
        ),
        name="guided_block",
    )(
        queries,
        self_keys,
        self_values,
        residual_in,
        text_keys.transpose(0, 1, 3, 2),
        text_values.transpose(0, 1, 3, 2),
        text_lengths,
        frame_counts,
        mod_gain.reshape(1, features),
        mod_shift.reshape(1, features),
        head_weight.T,
        head_bias.reshape(1, outs),
        guide_scale,
    )


def solution(mesh):
    return jax.shard_map(
        local,
        mesh=mesh,
        in_specs=(
            P(("parts", "seq"), None),
            P(("parts", "seq"), None),
            P(("parts", "seq"), None),
            P(("parts", "seq"), None),
            P(None, "parts", None, "seq"),
            P(None, "parts", None, "seq"),
            P(None, "parts"),
            P("parts"),
            P(),
            P(),
            P(),
            P(),
            P(),
        ),
        out_specs=P(("parts", "seq"), None),
        check_vma=False,
    )
```

```python
import functools
import math

import jax
import jax.numpy as jnp
from jax import lax
from jax.experimental import pallas as pl
from jax.experimental.pallas import tpu as pltpu
from jax.sharding import PartitionSpec as P

HEAD_CHANNELS = 128
TPF = 32
PENALTY = -1e30
EXP_SCALE = HEAD_CHANNELS ** (-0.5) * math.log2(math.e)
MESH_ID = pl.DeviceIdType.MESH


def inside(shape, dim, starts, ends):
    thin = tuple(1 if i == dim else size for i, size in enumerate(shape))
    feature = lax.broadcasted_iota(jnp.int32, thin, 1 - dim)
    low = jnp.zeros(thin, jnp.int32)
    high = jnp.zeros(thin, jnp.int32)
    for f, (start, end) in enumerate(zip(starts, ends)):
        low = jnp.where(feature == f, start, low)
        high = jnp.where(feature == f, end, high)
    place = lax.broadcasted_iota(jnp.int32, shape, dim)
    return (place >= low) & (place < high)


def weights_of(scores):
    top = jnp.max(scores, axis=-1, keepdims=True)
    raised = jnp.exp2((scores - top) * EXP_SCALE)
    total = jnp.sum(raised, axis=-1, keepdims=True)
    return (raised * (1.0 / total)).astype(jnp.bfloat16)


def kernel(
    n,
    q_ref,
    k_ref,
    v_ref,
    x_ref,
    tk_ref,
    tv_ref,
    lengths_ref,
    frames_ref,
    gain_ref,
    shift_ref,
    weight_ref,
    bias_ref,
    guide_ref,
    out_ref,
    qb,
    kb,
    vb,
    q_hot,
    keys,
    t_keys,
    t_vals_in,
    t_vals,
    p_self,
    cross,
    ob,
    att,
    xb,
    qkv_send,
    qkv_recv,
    pair_send,
    pair_recv,
    out_send,
    out_recv,
    here_sem,
):
    me = lax.axis_index("seq")
    chips = n // 2
    chip, core = me // 2, me % 2
    partner = chip * 2 + (1 - core)
    rows = q_ref.shape[0]
    half = rows // 2
    tokens = chips * rows
    videos = frames_ref.shape[0]
    share, text = tk_ref.shape[2:]
    paired = chips & (chips - 1) == 0

    def far_first(step):
        return chip ^ (chips - step) if paired else lax.rem(chip + step, chips)

    sources = (q_ref, k_ref, v_ref)
    landings = (qb, kb, vb)

    def block(index, size):
        return pl.ds(pl.multiple_of(index * size, size), size)

    def qkv_copy(which, peer):
        return pltpu.make_async_remote_copy(
            src_ref=sources[which].at[:, block(peer, HEAD_CHANNELS)],
            dst_ref=landings[which].at[block(chip, rows)],
            send_sem=qkv_send.at[which, peer],
            recv_sem=qkv_recv.at[which, chip],
            device_id={"seq": peer * 2 + core},
            device_id_type=MESH_ID,
        )

    def own_copy(which):
        return pltpu.make_async_copy(
            sources[which].at[:, block(chip, HEAD_CHANNELS)],
            landings[which].at[block(chip, rows)],
            qkv_recv.at[which, chip],
        )

    def qkv_wait(which, peer):
        place = landings[which].at[block(peer, rows)]
        pltpu.make_async_copy(place, place, qkv_recv.at[which, peer]).wait()

    key_place = t_keys.at[:, block(core, share), :]
    value_place = t_vals_in.at[:, block(core, share), :]
    pair_parts = (
        (tk_ref.at[1 - core], key_place),
        (tv_ref.at[1 - core], value_place),
        (x_ref.at[block(1 - core, half)], xb.at[core]),
    )
    here_parts = (
        (tk_ref.at[core], key_place),
        (tv_ref.at[core], value_place),
        (x_ref.at[block(core, half)], xb.at[core]),
    )
    pair_copies = [
        pltpu.make_async_remote_copy(
            src_ref=source,
            dst_ref=landing,
            send_sem=pair_send.at[i],
            recv_sem=pair_recv.at[i],
            device_id={"seq": partner},
            device_id_type=MESH_ID,
        )
        for i, (source, landing) in enumerate(pair_parts)
    ]
    here_copies = [
        pltpu.make_async_copy(source, landing, here_sem.at[i])
        for i, (source, landing) in enumerate(here_parts)
    ]

    barrier = pltpu.get_barrier_semaphore()

    @pl.loop(1, n)
    def _(step):
        pl.semaphore_signal(
            barrier, inc=1, device_id={"seq": lax.rem(me + step, n)}, device_id_type=MESH_ID
        )

    for copy in here_copies:
        copy.start()
    for which in range(3):
        own_copy(which).start()

    pl.semaphore_wait(barrier, n - 1)

    pair_copies[0].start()
    for which in range(3):

        @pl.loop(1, chips)
        def _(step, which=which):
            qkv_copy(which, far_first(step)).start()

        if which < 2:
            pair_copies[which + 1].start()

    starts, ends, position = [], [], jnp.int32(0)
    for f in range(videos):
        starts.append(position)
        position = position + frames_ref[f] * TPF
        ends.append(position)
    same = inside((tokens, HEAD_CHANNELS), 0, starts, ends)
    q_hot[...] = jnp.where(same, 1.0, 0.0).astype(jnp.bfloat16)
    apart = ~inside((HEAD_CHANNELS, tokens), 1, starts, ends)
    keys[HEAD_CHANNELS:, :] = jnp.where(apart, PENALTY, 0.0).astype(jnp.bfloat16)
    for f in range(videos):
        length = jnp.where(core == 0, lengths_ref[0, f], lengths_ref[1, f])
        live = inside(
            (HEAD_CHANNELS, text),
            1,
            [0] * videos,
            [length if other == f else 0 for other in range(videos)],
        )
        t_keys[f, HEAD_CHANNELS:, :] = jnp.where(live, 0.0, PENALTY).astype(jnp.bfloat16)

    def pair_wait(i):
        here_copies[i].wait()
        pair_copies[i].wait_recv()

    pair_wait(0)
    pair_wait(1)
    for f in range(videos):
        t_vals[f] = t_vals_in[f].T

    def query_block(index):
        place = block(index, rows)
        return jnp.concatenate([qb[place, :], q_hot[place, :]], axis=-1)

    def cross_of(index, queries):
        frames = rows // TPF
        picked = []
        for i in range(frames):
            frame = (index * frames + i) * TPF
            video = jnp.int32(0)
            for end in ends[:-1]:
                video = video + jnp.where(frame >= end, 1, 0)
            picked.append(video)
        parts = [slice(i * TPF, (i + 1) * TPF) for i in range(frames)]
        weights = weights_of(
            jnp.concatenate(
                [
                    jnp.dot(queries[part], t_keys[video], preferred_element_type=jnp.float32)
                    for part, video in zip(parts, picked)
                ],
                axis=0,
            )
        )
        return jnp.concatenate(
            [
                jnp.dot(weights[part], t_vals[video], preferred_element_type=jnp.float32)
                for part, video in zip(parts, picked)
            ],
            axis=0,
        )

    @pl.loop(0, chips)
    def _(step):
        index = lax.rem(chip + step, chips)
        qkv_wait(0, index)
        queries = query_block(index)
        cross[block(index, rows), :] = cross_of(index, queries)

    @pl.loop(0, chips)
    def _(step):
        qkv_wait(1, step)

    keys[:HEAD_CHANNELS, :] = kb[...].T

    @pl.loop(0, chips, unroll=4)
    def _(step):
        index = lax.rem(chip + step, chips)
        scores = jnp.dot(query_block(index), keys[...], preferred_element_type=jnp.float32)
        p_self[block(index, rows), :] = weights_of(scores)

    @pl.loop(0, chips)
    def _(step):
        qkv_wait(2, step)

    def out_copy(device):
        return pltpu.make_async_remote_copy(
            src_ref=ob.at[block(device, half)],
            dst_ref=att.at[core, :, block(chip, HEAD_CHANNELS)],
            send_sem=out_send.at[device],
            recv_sem=out_recv.at[me],
            device_id={"seq": device},
            device_id_type=MESH_ID,
        )

    def out_own():
        return pltpu.make_async_copy(
            ob.at[block(me, half)],
            att.at[core, :, block(chip, HEAD_CHANNELS)],
            out_recv.at[me],
        )

    @pl.loop(0, chips, unroll=4)
    def _(step):
        index = lax.rem(chip + 1 + step, chips)
        place = block(index, rows)
        mixed = cross[place, :] + jnp.dot(
            p_self[place, :], vb[...], preferred_element_type=jnp.float32
        )
        ob[place, :] = mixed.astype(jnp.bfloat16)
        for side in range(2):
            device = index * 2 + side

            @pl.when(device != me)
            def _():
                out_copy(device).start()

            @pl.when(device == me)
            def _():
                out_own().start()

    pair_wait(2)

    @pl.loop(0, n)
    def _(device):
        place = att.at[device % 2, :, block(device // 2, HEAD_CHANNELS)]
        pltpu.make_async_copy(place, place, out_recv.at[device]).wait()

    features = x_ref.shape[1]
    hidden = (xb[...].astype(jnp.float32) + att[...].astype(jnp.float32)).reshape(rows, features)
    centred = hidden - jnp.mean(hidden, axis=-1, keepdims=True)
    spread = jnp.mean(centred * centred, axis=-1, keepdims=True)
    normed = centred * lax.rsqrt(spread + 1e-06) * gain_ref[...] + shift_ref[...]
    velocity = (
        lax.dot_general(
            normed.astype(jnp.bfloat16),
            weight_ref[...],
            (((1,), (1,)), ((), ())),
            preferred_element_type=jnp.float32,
        )
        + bias_ref[...]
    )
    conditional, unconditional = velocity[:half], velocity[half:]
    out_ref[...] = unconditional + guide_ref[0] * (conditional - unconditional)

    for copy in pair_copies:
        copy.wait_send()
    for which in range(3):

        @pl.loop(1, chips)
        def _(step, which=which):
            qkv_copy(which, lax.rem(chip + step, chips)).wait_send()

    @pl.loop(1, n)
    def _(step):
        out_copy(lax.rem(me + step, n)).wait_send()


def local(
    queries,
    self_keys,
    self_values,
    residual_in,
    text_keys,
    text_values,
    text_lengths,
    frame_counts,
    mod_gain,
    mod_shift,
    head_weight,
    head_bias,
    guide_scale,
):
    n = lax.axis_size("seq")
    chips = n // 2
    rows, features = queries.shape
    half = rows // 2
    outs = head_weight.shape[1]
    tokens = chips * rows
    _, videos, text, _ = text_keys.shape
    bf16, f32 = jnp.bfloat16, jnp.float32
    anywhere = pl.BlockSpec(memory_space=pl.ANY)
    scalar = pl.BlockSpec(memory_space=pltpu.SMEM)
    vector = pl.BlockSpec(memory_space=pltpu.VMEM)
    return pl.pallas_call(
        functools.partial(kernel, n),
        out_shape=pltpu.VMEM((half, outs), f32),
        in_specs=[anywhere] * 6 + [scalar] * 2 + [vector] * 4 + [scalar],
        out_specs=vector,
        scratch_shapes=[
            pltpu.VMEM((tokens, HEAD_CHANNELS), bf16),
            pltpu.VMEM((tokens, HEAD_CHANNELS), bf16),
            pltpu.VMEM((tokens, HEAD_CHANNELS), bf16),
            pltpu.VMEM((tokens, HEAD_CHANNELS), bf16),
            pltpu.VMEM((2 * HEAD_CHANNELS, tokens), bf16),
            pltpu.VMEM((videos, 2 * HEAD_CHANNELS, text), bf16),
            pltpu.VMEM((videos, HEAD_CHANNELS, text), bf16),
            pltpu.VMEM((videos, text, HEAD_CHANNELS), bf16),
            pltpu.VMEM((tokens, tokens), bf16),
            pltpu.VMEM((tokens, HEAD_CHANNELS), f32),
            pltpu.VMEM((tokens, HEAD_CHANNELS), bf16),
            pltpu.VMEM((2, half, features), bf16),
            pltpu.VMEM((2, half, features), bf16),
            pltpu.SemaphoreType.DMA((3, chips)),
            pltpu.SemaphoreType.DMA((3, chips)),
            pltpu.SemaphoreType.DMA((3,)),
            pltpu.SemaphoreType.DMA((3,)),
            pltpu.SemaphoreType.DMA((n,)),
            pltpu.SemaphoreType.DMA((n,)),
            pltpu.SemaphoreType.DMA((3,)),
        ],
        compiler_params=pltpu.CompilerParams(
            collective_id=0, has_side_effects=True, vmem_limit_bytes=60 * 1024 * 1024
        ),
        name="guided_block",
    )(
        queries,
        self_keys,
        self_values,
        residual_in,
        text_keys.transpose(0, 1, 3, 2),
        text_values.transpose(0, 1, 3, 2),
        text_lengths,
        frame_counts,
        mod_gain.reshape(1, features),
        mod_shift.reshape(1, features),
        head_weight.T,
        head_bias.reshape(1, outs),
        guide_scale,
    )


def solution(mesh):
    return jax.shard_map(
        local,
        mesh=mesh,
        in_specs=(
            P(("parts", "seq"), None),
            P(("parts", "seq"), None),
            P(("parts", "seq"), None),
            P(("parts", "seq"), None),
            P(None, "parts", None, "seq"),
            P(None, "parts", None, "seq"),
            P(None, "parts"),
            P("parts"),
            P(),
            P(),
            P(),
            P(),
            P(),
        ),
        out_specs=P(("parts", "seq"), None),
        check_vma=False,
    )
```

```python
import functools
import math

import jax
import jax.numpy as jnp
from jax import lax
from jax.experimental import pallas as pl
from jax.experimental.pallas import tpu as pltpu
from jax.sharding import PartitionSpec as P

HEAD_CHANNELS = 128
TPF = 32
PENALTY = -1e30
EXP_SCALE = HEAD_CHANNELS ** (-0.5) * math.log2(math.e)
MESH_ID = pl.DeviceIdType.MESH


def inside(shape, dim, starts, ends):
    thin = tuple(1 if i == dim else size for i, size in enumerate(shape))
    feature = lax.broadcasted_iota(jnp.int32, thin, 1 - dim)
    low = jnp.zeros(thin, jnp.int32)
    high = jnp.zeros(thin, jnp.int32)
    for f, (start, end) in enumerate(zip(starts, ends)):
        low = jnp.where(feature == f, start, low)
        high = jnp.where(feature == f, end, high)
    place = lax.broadcasted_iota(jnp.int32, shape, dim)
    return (place >= low) & (place < high)


def weights_of(scores):
    top = jnp.max(scores, axis=-1, keepdims=True)
    raised = jnp.exp2((scores - top) * EXP_SCALE)
    total = jnp.sum(raised, axis=-1, keepdims=True)
    return (raised * (1.0 / total)).astype(jnp.bfloat16)


def kernel(
    n,
    q_ref,
    k_ref,
    v_ref,
    x_ref,
    tk_ref,
    tv_ref,
    lengths_ref,
    frames_ref,
    gain_ref,
    shift_ref,
    weight_ref,
    bias_ref,
    guide_ref,
    out_ref,
    qb,
    kb,
    vb,
    q_hot,
    keys,
    t_keys,
    t_vals_in,
    t_vals,
    p_self,
    cross,
    ob,
    att,
    xb,
    qkv_send,
    qkv_recv,
    pair_send,
    pair_recv,
    out_send,
    out_recv,
    here_sem,
    late_sem,
):
    me = lax.axis_index("seq")
    chips = n // 2
    chip, core = me // 2, me % 2
    partner = chip * 2 + (1 - core)
    rows = q_ref.shape[0]
    half = rows // 2
    tokens = chips * rows
    videos = frames_ref.shape[0]
    share, text = tk_ref.shape[2:]
    paired = chips & (chips - 1) == 0

    def far_first(step):
        return chip ^ (chips - step) if paired else lax.rem(chip + step, chips)

    sources = (q_ref, k_ref, v_ref)
    landings = (qb, kb, vb)

    def block(index, size):
        return pl.ds(pl.multiple_of(index * size, size), size)

    def qkv_copy(which, peer):
        return pltpu.make_async_remote_copy(
            src_ref=sources[which].at[:, block(peer, HEAD_CHANNELS)],
            dst_ref=landings[which].at[block(chip, rows)],
            send_sem=qkv_send.at[which, peer],
            recv_sem=qkv_recv.at[which, chip],
            device_id={"seq": peer * 2 + core},
            device_id_type=MESH_ID,
        )

    def own_copy(which):
        return pltpu.make_async_copy(
            sources[which].at[:, block(chip, HEAD_CHANNELS)],
            landings[which].at[block(chip, rows)],
            qkv_recv.at[which, chip],
        )

    def qkv_wait(which, peer):
        place = landings[which].at[block(peer, rows)]
        pltpu.make_async_copy(place, place, qkv_recv.at[which, peer]).wait()

    key_place = t_keys.at[:, block(core, share), :]
    value_place = t_vals_in.at[:, block(core, share), :]
    pair_parts = (
        (tk_ref.at[1 - core], key_place),
        (tv_ref.at[1 - core], value_place),
        (x_ref.at[block(1 - core, half)], xb.at[core]),
    )
    here_parts = (
        (tk_ref.at[core], key_place),
        (tv_ref.at[core], value_place),
        (x_ref.at[block(core, half)], xb.at[core]),
    )
    pair_copies = [
        pltpu.make_async_remote_copy(
            src_ref=source,
            dst_ref=landing,
            send_sem=pair_send.at[i],
            recv_sem=pair_recv.at[i],
            device_id={"seq": partner},
            device_id_type=MESH_ID,
        )
        for i, (source, landing) in enumerate(pair_parts)
    ]
    here_copies = [
        pltpu.make_async_copy(source, landing, here_sem.at[i])
        for i, (source, landing) in enumerate(here_parts)
    ]

    barrier = pltpu.get_barrier_semaphore()

    early = (chips - chips // 4) * 2
    is_early = me < early

    def greet(semaphore, device):
        pl.semaphore_signal(
            semaphore, inc=1, device_id={"seq": device}, device_id_type=MESH_ID
        )

    @pl.when(is_early)
    def _():
        @pl.loop(1, n)
        def _(step):
            greet(barrier, lax.rem(me + step, n))

    @pl.when(jnp.logical_not(is_early))
    def _():
        @pl.loop(early, n)
        def _(device):
            @pl.when(device != me)
            def _():
                greet(barrier, device)

    for copy in here_copies:
        copy.start()
    for which in range(3):
        own_copy(which).start()

    def send_all(which):
        @pl.loop(1, chips)
        def _(step):
            qkv_copy(which, far_first(step)).start()

    def send_group(which, to_early):
        @pl.loop(1, chips)
        def _(step):
            peer = far_first(step)

            @pl.when((peer * 2 < early) == to_early)
            def _():
                qkv_copy(which, peer).start()

    @pl.when(is_early)
    def _():
        pl.semaphore_wait(barrier, early - 1)
        pair_copies[0].start()
        for which in range(1):
            send_group(which, True)
        pair_copies[1].start()

    @pl.when(jnp.logical_not(is_early))
    def _():
        pl.semaphore_wait(barrier, n - 1)

        @pl.loop(0, early)
        def _(device):
            greet(late_sem, device)

        pair_copies[0].start()
        for which in range(1):
            send_all(which)
        pair_copies[1].start()

    starts, ends, position = [], [], jnp.int32(0)
    for f in range(videos):
        starts.append(position)
        position = position + frames_ref[f] * TPF
        ends.append(position)
    same = inside((tokens, HEAD_CHANNELS), 0, starts, ends)
    q_hot[...] = jnp.where(same, 1.0, 0.0).astype(jnp.bfloat16)
    apart = ~inside((HEAD_CHANNELS, tokens), 1, starts, ends)
    keys[HEAD_CHANNELS:, :] = jnp.where(apart, PENALTY, 0.0).astype(jnp.bfloat16)
    for f in range(videos):
        length = jnp.where(core == 0, lengths_ref[0, f], lengths_ref[1, f])
        live = inside(
            (HEAD_CHANNELS, text),
            1,
            [0] * videos,
            [length if other == f else 0 for other in range(videos)],
        )
        t_keys[f, HEAD_CHANNELS:, :] = jnp.where(live, 0.0, PENALTY).astype(jnp.bfloat16)

    def pair_wait(i):
        here_copies[i].wait()
        pair_copies[i].wait_recv()

    @pl.when(is_early)
    def _():
        pl.semaphore_wait(late_sem, n - early)
        for which in range(1):
            send_group(which, False)

    for which in range(1, 3):
        send_all(which)
    pair_copies[2].start()

    pair_wait(0)
    pair_wait(1)
    for f in range(videos):
        t_vals[f] = t_vals_in[f].T

    def query_block(index):
        place = block(index, rows)
        return jnp.concatenate([qb[place, :], q_hot[place, :]], axis=-1)

    def cross_of(index, queries):
        frames = rows // TPF
        picked = []
        for i in range(frames):
            frame = (index * frames + i) * TPF
            video = jnp.int32(0)
            for end in ends[:-1]:
                video = video + jnp.where(frame >= end, 1, 0)
            picked.append(video)
        parts = [slice(i * TPF, (i + 1) * TPF) for i in range(frames)]
        weights = weights_of(
            jnp.concatenate(
                [
                    jnp.dot(queries[part], t_keys[video], preferred_element_type=jnp.float32)
                    for part, video in zip(parts, picked)
                ],
                axis=0,
            )
        )
        return jnp.concatenate(
            [
                jnp.dot(weights[part], t_vals[video], preferred_element_type=jnp.float32)
                for part, video in zip(parts, picked)
            ],
            axis=0,
        )

    @pl.loop(0, chips)
    def _(step):
        index = lax.rem(chip + step, chips)
        qkv_wait(0, index)
        queries = query_block(index)
        cross[block(index, rows), :] = cross_of(index, queries)

    @pl.loop(0, chips)
    def _(step):
        qkv_wait(1, step)

    keys[:HEAD_CHANNELS, :] = kb[...].T

    @pl.loop(0, chips, unroll=4)
    def _(step):
        index = lax.rem(chip + step, chips)
        scores = jnp.dot(query_block(index), keys[...], preferred_element_type=jnp.float32)
        p_self[block(index, rows), :] = weights_of(scores)

    @pl.loop(0, chips)
    def _(step):
        qkv_wait(2, step)

    def out_copy(device):
        return pltpu.make_async_remote_copy(
            src_ref=ob.at[block(device, half)],
            dst_ref=att.at[core, :, block(chip, HEAD_CHANNELS)],
            send_sem=out_send.at[device],
            recv_sem=out_recv.at[me],
            device_id={"seq": device},
            device_id_type=MESH_ID,
        )

    def out_own():
        return pltpu.make_async_copy(
            ob.at[block(me, half)],
            att.at[core, :, block(chip, HEAD_CHANNELS)],
            out_recv.at[me],
        )

    @pl.loop(0, chips, unroll=4)
    def _(step):
        index = lax.rem(chip + 1 + step, chips)
        place = block(index, rows)
        mixed = cross[place, :] + jnp.dot(
            p_self[place, :], vb[...], preferred_element_type=jnp.float32
        )
        ob[place, :] = mixed.astype(jnp.bfloat16)
        for side in range(2):
            device = index * 2 + side

            @pl.when(device != me)
            def _():
                out_copy(device).start()

            @pl.when(device == me)
            def _():
                out_own().start()

    pair_wait(2)

    @pl.loop(0, n)
    def _(device):
        place = att.at[device % 2, :, block(device // 2, HEAD_CHANNELS)]
        pltpu.make_async_copy(place, place, out_recv.at[device]).wait()

    features = x_ref.shape[1]
    hidden = (xb[...].astype(jnp.float32) + att[...].astype(jnp.float32)).reshape(rows, features)
    centred = hidden - jnp.mean(hidden, axis=-1, keepdims=True)
    spread = jnp.mean(centred * centred, axis=-1, keepdims=True)
    normed = centred * lax.rsqrt(spread + 1e-06) * gain_ref[...] + shift_ref[...]
    velocity = (
        lax.dot_general(
            normed.astype(jnp.bfloat16),
            weight_ref[...],
            (((1,), (1,)), ((), ())),
            preferred_element_type=jnp.float32,
        )
        + bias_ref[...]
    )
    conditional, unconditional = velocity[:half], velocity[half:]
    out_ref[...] = unconditional + guide_ref[0] * (conditional - unconditional)

    for copy in pair_copies:
        copy.wait_send()
    for which in range(3):

        @pl.loop(1, chips)
        def _(step, which=which):
            qkv_copy(which, lax.rem(chip + step, chips)).wait_send()

    @pl.loop(1, n)
    def _(step):
        out_copy(lax.rem(me + step, n)).wait_send()


def local(
    queries,
    self_keys,
    self_values,
    residual_in,
    text_keys,
    text_values,
    text_lengths,
    frame_counts,
    mod_gain,
    mod_shift,
    head_weight,
    head_bias,
    guide_scale,
):
    n = lax.axis_size("seq")
    chips = n // 2
    rows, features = queries.shape
    half = rows // 2
    outs = head_weight.shape[1]
    tokens = chips * rows
    _, videos, text, _ = text_keys.shape
    bf16, f32 = jnp.bfloat16, jnp.float32
    anywhere = pl.BlockSpec(memory_space=pl.ANY)
    scalar = pl.BlockSpec(memory_space=pltpu.SMEM)
    vector = pl.BlockSpec(memory_space=pltpu.VMEM)
    return pl.pallas_call(
        functools.partial(kernel, n),
        out_shape=pltpu.VMEM((half, outs), f32),
        in_specs=[anywhere] * 6 + [scalar] * 2 + [vector] * 4 + [scalar],
        out_specs=vector,
        scratch_shapes=[
            pltpu.VMEM((tokens, HEAD_CHANNELS), bf16),
            pltpu.VMEM((tokens, HEAD_CHANNELS), bf16),
            pltpu.VMEM((tokens, HEAD_CHANNELS), bf16),
            pltpu.VMEM((tokens, HEAD_CHANNELS), bf16),
            pltpu.VMEM((2 * HEAD_CHANNELS, tokens), bf16),
            pltpu.VMEM((videos, 2 * HEAD_CHANNELS, text), bf16),
            pltpu.VMEM((videos, HEAD_CHANNELS, text), bf16),
            pltpu.VMEM((videos, text, HEAD_CHANNELS), bf16),
            pltpu.VMEM((tokens, tokens), bf16),
            pltpu.VMEM((tokens, HEAD_CHANNELS), f32),
            pltpu.VMEM((tokens, HEAD_CHANNELS), bf16),
            pltpu.VMEM((2, half, features), bf16),
            pltpu.VMEM((2, half, features), bf16),
            pltpu.SemaphoreType.DMA((3, chips)),
            pltpu.SemaphoreType.DMA((3, chips)),
            pltpu.SemaphoreType.DMA((3,)),
            pltpu.SemaphoreType.DMA((3,)),
            pltpu.SemaphoreType.DMA((n,)),
            pltpu.SemaphoreType.DMA((n,)),
            pltpu.SemaphoreType.DMA((3,)),
            pltpu.SemaphoreType.REGULAR,
        ],
        compiler_params=pltpu.CompilerParams(
            collective_id=0, has_side_effects=True, vmem_limit_bytes=60 * 1024 * 1024
        ),
        name="guided_block",
    )(
        queries,
        self_keys,
        self_values,
        residual_in,
        text_keys.transpose(0, 1, 3, 2),
        text_values.transpose(0, 1, 3, 2),
        text_lengths,
        frame_counts,
        mod_gain.reshape(1, features),
        mod_shift.reshape(1, features),
        head_weight.T,
        head_bias.reshape(1, outs),
        guide_scale,
    )


def solution(mesh):
    return jax.shard_map(
        local,
        mesh=mesh,
        in_specs=(
            P(("parts", "seq"), None),
            P(("parts", "seq"), None),
            P(("parts", "seq"), None),
            P(("parts", "seq"), None),
            P(None, "parts", None, "seq"),
            P(None, "parts", None, "seq"),
            P(None, "parts"),
            P("parts"),
            P(),
            P(),
            P(),
            P(),
            P(),
        ),
        out_specs=P(("parts", "seq"), None),
        check_vma=False,
    )
```

```python
import functools
import math

import jax
import jax.numpy as jnp
from jax import lax
from jax.experimental import pallas as pl
from jax.experimental.pallas import tpu as pltpu
from jax.sharding import PartitionSpec as P

HEAD_CHANNELS = 128
TPF = 32
PENALTY = -1e30
EXP_SCALE = HEAD_CHANNELS ** (-0.5) * math.log2(math.e)
MESH_ID = pl.DeviceIdType.MESH


def inside(shape, dim, starts, ends):
    thin = tuple(1 if i == dim else size for i, size in enumerate(shape))
    feature = lax.broadcasted_iota(jnp.int32, thin, 1 - dim)
    low = jnp.zeros(thin, jnp.int32)
    high = jnp.zeros(thin, jnp.int32)
    for f, (start, end) in enumerate(zip(starts, ends)):
        low = jnp.where(feature == f, start, low)
        high = jnp.where(feature == f, end, high)
    place = lax.broadcasted_iota(jnp.int32, shape, dim)
    return (place >= low) & (place < high)


def weights_of(scores):
    top = jnp.max(scores, axis=-1, keepdims=True)
    raised = jnp.exp2((scores - top) * EXP_SCALE)
    total = jnp.sum(raised, axis=-1, keepdims=True)
    return (raised * (1.0 / total)).astype(jnp.bfloat16)


def kernel(
    n,
    q_ref,
    k_ref,
    v_ref,
    x_ref,
    tk_ref,
    tv_ref,
    lengths_ref,
    frames_ref,
    gain_ref,
    shift_ref,
    weight_ref,
    bias_ref,
    guide_ref,
    out_ref,
    qb,
    kb,
    vb,
    q_hot,
    keys,
    t_keys,
    t_vals_in,
    t_vals,
    p_self,
    cross,
    ob,
    att,
    xb,
    qkv_send,
    qkv_recv,
    pair_send,
    pair_recv,
    out_send,
    out_recv,
    here_sem,
    late_sem,
    weight_here,
):
    me = lax.axis_index("seq")
    chips = n // 2
    chip, core = me // 2, me % 2
    partner = chip * 2 + (1 - core)
    rows = q_ref.shape[0]
    half = rows // 2
    tokens = chips * rows
    videos = frames_ref.shape[0]
    share, text = tk_ref.shape[2:]
    paired = chips & (chips - 1) == 0

    def far_first(step):
        return chip ^ (chips - step) if paired else lax.rem(chip + step, chips)

    sources = (q_ref, k_ref, v_ref)
    landings = (qb, kb, vb)

    def block(index, size):
        return pl.ds(pl.multiple_of(index * size, size), size)

    def qkv_copy(which, peer):
        return pltpu.make_async_remote_copy(
            src_ref=sources[which].at[:, block(peer, HEAD_CHANNELS)],
            dst_ref=landings[which].at[block(chip, rows)],
            send_sem=qkv_send.at[which, peer],
            recv_sem=qkv_recv.at[which, chip],
            device_id={"seq": peer * 2 + core},
            device_id_type=MESH_ID,
        )

    def own_copy(which):
        return pltpu.make_async_copy(
            sources[which].at[:, block(chip, HEAD_CHANNELS)],
            landings[which].at[block(chip, rows)],
            qkv_recv.at[which, chip],
        )

    def qkv_wait(which, peer):
        place = landings[which].at[block(peer, rows)]
        pltpu.make_async_copy(place, place, qkv_recv.at[which, peer]).wait()

    key_place = t_keys.at[:, block(core, share), :]
    value_place = t_vals_in.at[:, block(core, share), :]
    pair_parts = (
        (tk_ref.at[1 - core], key_place),
        (tv_ref.at[1 - core], value_place),
        (x_ref.at[block(1 - core, half)], xb.at[core]),
    )
    here_parts = (
        (tk_ref.at[core], key_place),
        (tv_ref.at[core], value_place),
        (x_ref.at[block(core, half)], xb.at[core]),
        (weight_ref, weight_here),
    )
    pair_copies = [
        pltpu.make_async_remote_copy(
            src_ref=source,
            dst_ref=landing,
            send_sem=pair_send.at[i],
            recv_sem=pair_recv.at[i],
            device_id={"seq": partner},
            device_id_type=MESH_ID,
        )
        for i, (source, landing) in enumerate(pair_parts)
    ]
    here_copies = [
        pltpu.make_async_copy(source, landing, here_sem.at[i])
        for i, (source, landing) in enumerate(here_parts)
    ]

    barrier = pltpu.get_barrier_semaphore()

    early = (chips - chips // 4) * 2
    is_early = me < early

    def greet(semaphore, device):
        pl.semaphore_signal(
            semaphore, inc=1, device_id={"seq": device}, device_id_type=MESH_ID
        )

    @pl.when(is_early)
    def _():
        @pl.loop(1, n)
        def _(step):
            greet(barrier, lax.rem(me + step, n))

    @pl.when(jnp.logical_not(is_early))
    def _():
        @pl.loop(early, n)
        def _(device):
            @pl.when(device != me)
            def _():
                greet(barrier, device)

    for copy in here_copies:
        copy.start()
    for which in range(3):
        own_copy(which).start()

    def send_all(which):
        @pl.loop(1, chips)
        def _(step):
            qkv_copy(which, far_first(step)).start()

    def send_group(which, to_early):
        @pl.loop(1, chips)
        def _(step):
            peer = far_first(step)

            @pl.when((peer * 2 < early) == to_early)
            def _():
                qkv_copy(which, peer).start()

    @pl.when(is_early)
    def _():
        pl.semaphore_wait(barrier, early - 1)
        pair_copies[0].start()
        for which in range(1):
            send_group(which, True)
        pair_copies[1].start()

    @pl.when(jnp.logical_not(is_early))
    def _():
        pl.semaphore_wait(barrier, n - 1)

        @pl.loop(0, early)
        def _(device):
            greet(late_sem, device)

        pair_copies[0].start()
        for which in range(1):
            send_all(which)
        pair_copies[1].start()

    starts, ends, position = [], [], jnp.int32(0)
    for f in range(videos):
        starts.append(position)
        position = position + frames_ref[f] * TPF
        ends.append(position)
    same = inside((tokens, HEAD_CHANNELS), 0, starts, ends)
    q_hot[...] = jnp.where(same, 1.0, 0.0).astype(jnp.bfloat16)
    apart = ~inside((HEAD_CHANNELS, tokens), 1, starts, ends)
    keys[HEAD_CHANNELS:, :] = jnp.where(apart, PENALTY, 0.0).astype(jnp.bfloat16)
    for f in range(videos):
        length = jnp.where(core == 0, lengths_ref[0, f], lengths_ref[1, f])
        live = inside(
            (HEAD_CHANNELS, text),
            1,
            [0] * videos,
            [length if other == f else 0 for other in range(videos)],
        )
        t_keys[f, HEAD_CHANNELS:, :] = jnp.where(live, 0.0, PENALTY).astype(jnp.bfloat16)

    def pair_wait(i):
        here_copies[i].wait()
        pair_copies[i].wait_recv()

    @pl.when(is_early)
    def _():
        pl.semaphore_wait(late_sem, n - early)
        for which in range(1):
            send_group(which, False)

    for which in range(1, 3):
        send_all(which)
    pair_copies[2].start()

    pair_wait(0)
    pair_wait(1)
    for f in range(videos):
        t_vals[f] = t_vals_in[f].T

    def query_block(index):
        place = block(index, rows)
        return jnp.concatenate([qb[place, :], q_hot[place, :]], axis=-1)

    def cross_of(index, queries):
        frames = rows // TPF
        picked = []
        for i in range(frames):
            frame = (index * frames + i) * TPF
            video = jnp.int32(0)
            for end in ends[:-1]:
                video = video + jnp.where(frame >= end, 1, 0)
            picked.append(video)
        parts = [slice(i * TPF, (i + 1) * TPF) for i in range(frames)]
        weights = weights_of(
            jnp.concatenate(
                [
                    jnp.dot(queries[part], t_keys[video], preferred_element_type=jnp.float32)
                    for part, video in zip(parts, picked)
                ],
                axis=0,
            )
        )
        return jnp.concatenate(
            [
                jnp.dot(weights[part], t_vals[video], preferred_element_type=jnp.float32)
                for part, video in zip(parts, picked)
            ],
            axis=0,
        )

    @pl.loop(0, chips)
    def _(step):
        index = lax.rem(chip + step, chips)
        qkv_wait(0, index)
        queries = query_block(index)
        cross[block(index, rows), :] = cross_of(index, queries)

    @pl.loop(0, chips)
    def _(step):
        qkv_wait(1, step)

    keys[:HEAD_CHANNELS, :] = kb[...].T

    @pl.loop(0, chips, unroll=4)
    def _(step):
        index = lax.rem(chip + step, chips)
        scores = jnp.dot(query_block(index), keys[...], preferred_element_type=jnp.float32)
        p_self[block(index, rows), :] = weights_of(scores)

    @pl.loop(0, chips)
    def _(step):
        qkv_wait(2, step)

    def out_copy(device):
        return pltpu.make_async_remote_copy(
            src_ref=ob.at[block(device, half)],
            dst_ref=att.at[core, :, block(chip, HEAD_CHANNELS)],
            send_sem=out_send.at[device],
            recv_sem=out_recv.at[me],
            device_id={"seq": device},
            device_id_type=MESH_ID,
        )

    def out_own():
        return pltpu.make_async_copy(
            ob.at[block(me, half)],
            att.at[core, :, block(chip, HEAD_CHANNELS)],
            out_recv.at[me],
        )

    @pl.loop(0, chips, unroll=4)
    def _(step):
        index = lax.rem(chip + 1 + step, chips)
        place = block(index, rows)
        mixed = cross[place, :] + jnp.dot(
            p_self[place, :], vb[...], preferred_element_type=jnp.float32
        )
        ob[place, :] = mixed.astype(jnp.bfloat16)
        for side in range(2):
            device = index * 2 + side

            @pl.when(device != me)
            def _():
                out_copy(device).start()

            @pl.when(device == me)
            def _():
                out_own().start()

    pair_wait(2)
    here_copies[3].wait()

    @pl.loop(0, n)
    def _(device):
        place = att.at[device % 2, :, block(device // 2, HEAD_CHANNELS)]
        pltpu.make_async_copy(place, place, out_recv.at[device]).wait()

    features = x_ref.shape[1]
    hidden = (xb[...].astype(jnp.float32) + att[...].astype(jnp.float32)).reshape(rows, features)
    centred = hidden - jnp.mean(hidden, axis=-1, keepdims=True)
    spread = jnp.mean(centred * centred, axis=-1, keepdims=True)
    normed = centred * lax.rsqrt(spread + 1e-06) * gain_ref[...] + shift_ref[...]
    velocity = (
        lax.dot_general(
            normed.astype(jnp.bfloat16),
            weight_here[...],
            (((1,), (1,)), ((), ())),
            preferred_element_type=jnp.float32,
        )
        + bias_ref[...]
    )
    conditional, unconditional = velocity[:half], velocity[half:]
    out_ref[...] = unconditional + guide_ref[0] * (conditional - unconditional)

    for copy in pair_copies:
        copy.wait_send()
    for which in range(3):

        @pl.loop(1, chips)
        def _(step, which=which):
            qkv_copy(which, lax.rem(chip + step, chips)).wait_send()

    @pl.loop(1, n)
    def _(step):
        out_copy(lax.rem(me + step, n)).wait_send()


def local(
    queries,
    self_keys,
    self_values,
    residual_in,
    text_keys,
    text_values,
    text_lengths,
    frame_counts,
    mod_gain,
    mod_shift,
    head_weight,
    head_bias,
    guide_scale,
):
    n = lax.axis_size("seq")
    chips = n // 2
    rows, features = queries.shape
    half = rows // 2
    outs = head_weight.shape[1]
    tokens = chips * rows
    _, videos, text, _ = text_keys.shape
    bf16, f32 = jnp.bfloat16, jnp.float32
    anywhere = pl.BlockSpec(memory_space=pl.ANY)
    scalar = pl.BlockSpec(memory_space=pltpu.SMEM)
    vector = pl.BlockSpec(memory_space=pltpu.VMEM)
    return pl.pallas_call(
        functools.partial(kernel, n),
        out_shape=pltpu.VMEM((half, outs), f32),
        in_specs=[anywhere] * 6 + [scalar] * 2 + [vector] * 2 + [anywhere] + [vector] + [scalar],
        out_specs=vector,
        scratch_shapes=[
            pltpu.VMEM((tokens, HEAD_CHANNELS), bf16),
            pltpu.VMEM((tokens, HEAD_CHANNELS), bf16),
            pltpu.VMEM((tokens, HEAD_CHANNELS), bf16),
            pltpu.VMEM((tokens, HEAD_CHANNELS), bf16),
            pltpu.VMEM((2 * HEAD_CHANNELS, tokens), bf16),
            pltpu.VMEM((videos, 2 * HEAD_CHANNELS, text), bf16),
            pltpu.VMEM((videos, HEAD_CHANNELS, text), bf16),
            pltpu.VMEM((videos, text, HEAD_CHANNELS), bf16),
            pltpu.VMEM((tokens, tokens), bf16),
            pltpu.VMEM((tokens, HEAD_CHANNELS), f32),
            pltpu.VMEM((tokens, HEAD_CHANNELS), bf16),
            pltpu.VMEM((2, half, features), bf16),
            pltpu.VMEM((2, half, features), bf16),
            pltpu.SemaphoreType.DMA((3, chips)),
            pltpu.SemaphoreType.DMA((3, chips)),
            pltpu.SemaphoreType.DMA((3,)),
            pltpu.SemaphoreType.DMA((3,)),
            pltpu.SemaphoreType.DMA((n,)),
            pltpu.SemaphoreType.DMA((n,)),
            pltpu.SemaphoreType.DMA((4,)),
            pltpu.SemaphoreType.REGULAR,
            pltpu.VMEM((outs, features), bf16),
        ],
        compiler_params=pltpu.CompilerParams(
            collective_id=0, has_side_effects=True, vmem_limit_bytes=60 * 1024 * 1024
        ),
        name="guided_block",
    )(
        queries,
        self_keys,
        self_values,
        residual_in,
        text_keys.transpose(0, 1, 3, 2),
        text_values.transpose(0, 1, 3, 2),
        text_lengths,
        frame_counts,
        mod_gain.reshape(1, features),
        mod_shift.reshape(1, features),
        head_weight.T,
        head_bias.reshape(1, outs),
        guide_scale,
    )


def solution(mesh):
    return jax.shard_map(
        local,
        mesh=mesh,
        in_specs=(
            P(("parts", "seq"), None),
            P(("parts", "seq"), None),
            P(("parts", "seq"), None),
            P(("parts", "seq"), None),
            P(None, "parts", None, "seq"),
            P(None, "parts", None, "seq"),
            P(None, "parts"),
            P("parts"),
            P(),
            P(),
            P(),
            P(),
            P(),
        ),
        out_specs=P(("parts", "seq"), None),
        check_vma=False,
    )
```
